32 devices in a mesh: ta: 4 (over y, x), ha: 2 (over core), head: 4 (over z).
Axes of the slice: x: 2, y: 2, z: 4, core: 2. Of those that a mesh axis runs over, the one named last changes fastest.
Arguments:
- queries: bfloat16 [24, 16, 8, 2048], P('ta', ('ha', 'head')), may hold values from -90 to 90
- keys: bfloat16 [24, 16, 8, 2048], P('ta', ('ha', 'head')), may hold values from -4.5 to 4.5
- values: bfloat16 [24, 16, 8, 2048], P('ta', ('ha', 'head')), may hold values from -6 to 6
- out_grad: bfloat16 [24, 16, 8, 2048], P('ta', ('ha', 'head')), may hold values from -6 to 6
Outputs:
- attended: bfloat16 [24, 16, 8, 2048], P('ta', ('ha', 'head'))
- query_grad: bfloat16 [24, 16, 8, 2048], P('ta', ('ha', 'head'))
- key_grad: bfloat16 [24, 16, 8, 2048], P('ta', ('ha', 'head'))
- value_grad: bfloat16 [24, 16, 8, 2048], P('ta', ('ha', 'head'))
The draws below stay inside these ranges and needn't reach their ends.
All inputs are finite; a program needn't handle non-finite values.
Results may differ from the reference program's by a relative error of at most 0.025.
Values may be sent and summed in bfloat16 or wider, within the bound.
A program may use at most 128 MiB of HBM per device.

```python
import math
import jax
import jax.numpy as jnp
from jax import lax

TT = 6
TH = 8
W = 8
HEADS = 16
DH = 128
NT = 24
NH = 16
CH = 2048


def pair_draw(key):
    shape = (NT * NH * W, CH)
    key_flat = jnp.clip(jax.random.normal(jax.random.fold_in(key, 21), shape, jnp.float32), -4.0, 4.0)
    query_flat = jnp.clip(jax.random.normal(jax.random.fold_in(key, 22), shape, jnp.float32), -4.0, 4.0)
    return (query_flat.reshape(NT, NH, W, CH), key_flat.reshape(NT, NH, W, CH))


def draw_queries(key, part):
    return pair_draw(key)[0].astype(jnp.bfloat16)


def draw_keys(key, part):
    return pair_draw(key)[1].astype(jnp.bfloat16)


def shard_levels(stream_key, shape, split, least, largest):
    loudness, own = 1.0, jax.random.fold_in(stream_key, 6)
    for dim, shards_of in split:
        heights = jnp.exp(jax.random.uniform(jax.random.fold_in(own, dim), (shards_of,), jnp.float32, least / len(split), largest / len(split)))
        loudness = loudness * jnp.repeat(heights, shape[dim] // shards_of).reshape([-1 if axis == dim else 1 for axis in range(len(shape))])
    return loudness


def gaussian(key, shape, spread, limit, pieces=(), kind=jnp.bfloat16):
    values = jax.random.normal(key, shape, jnp.float32) * spread
    if len(pieces) > 0:
        values = shard_levels(key, shape, pieces, -0.22, 0.18) * values
    return jnp.clip(values, min=-limit, max=limit).astype(kind)


def setup_inputs(seed: int = 0) -> dict:
    key_of = jax.random.split(jax.random.key(seed), 5)
    return {
        "queries": draw_queries(jax.random.fold_in(key_of[4], 71), 0),
        "keys": draw_keys(jax.random.fold_in(key_of[4], 71), 0),
        "values": gaussian(key_of[2], (NT, NH, W, CH), 1.0, 6.0, ((0, 4), (1, 8))),
        "out_grad": gaussian(key_of[3], (NT, NH, W, CH), 1.0, 6.0, ((0, 4), (1, 8))),
    }


def to_blocks(array, count_t, count_h, columns):
    shaped = array.reshape(count_t, TT, count_h, TH, columns, HEADS, DH)
    return shaped.transpose(0, 2, 5, 1, 3, 4, 6).reshape(count_t, count_h, HEADS, TT * TH * columns, DH)

def from_blocks(array, count_t, count_h, columns):
    shaped = array.reshape(count_t, count_h, HEADS, TT, TH, columns, DH)
    return shaped.transpose(0, 3, 1, 4, 5, 2, 6).reshape(count_t * TT, count_h * TH, columns, HEADS * DH)

def pad_tiles(array):
    return jnp.pad(array, ((1, 1), (1, 1)) + ((0, 0),) * (array.ndim - 2))

def beside_all(padded, first, second):
    zero = jnp.zeros((), jnp.int32)
    starts = (first.astype(jnp.int32), second.astype(jnp.int32)) + (zero,) * (padded.ndim - 2)
    sizes = (3, 3) + padded.shape[2:]
    piece = lax.dynamic_slice(padded, starts, sizes)
    moved = jnp.moveaxis(piece, 2, 0)
    return moved.reshape((HEADS, 9 * padded.shape[3]) + padded.shape[4:])

def window(first, second, count_t, count_h, tokens):
    offsets = jnp.arange(3, dtype=jnp.int32) - 1
    time_valid = (first + offsets >= 0) & (first + offsets < count_t)
    row_valid = (second + offsets >= 0) & (second + offsets < count_h)
    key_valid = jnp.repeat((time_valid[:, None] & row_valid[None, :]).reshape(9), tokens)
    return key_valid[None, :]

def reference(queries, keys, values, out_grad):
    count_t = queries.shape[0] // TT
    count_h = queries.shape[1] // TH
    columns = queries.shape[2]
    tokens = TT * TH * columns
    factor = 1.0 / math.sqrt(DH)
    query_blocks = to_blocks(queries, count_t, count_h, columns)
    key_blocks = to_blocks(keys, count_t, count_h, columns)
    value_blocks = to_blocks(values, count_t, count_h, columns)
    grad_blocks = to_blocks(out_grad, count_t, count_h, columns)
    key_pad = pad_tiles(key_blocks)
    value_pad = pad_tiles(value_blocks)

    def forward(index):
        first = index // count_h
        second = index % count_h
        allowed = window(first, second, count_t, count_h, tokens)
        own_q = query_blocks[first, second].astype(jnp.float32)
        own_g = grad_blocks[first, second].astype(jnp.float32)
        near_k = beside_all(key_pad, first, second).astype(jnp.float32)
        near_v = beside_all(value_pad, first, second).astype(jnp.float32)
        scores = jnp.einsum('hqd,hkd->hqk', own_q, near_k) * factor
        scores = jnp.where(allowed[None], scores, -jnp.inf)
        highest = lax.optimization_barrier(jnp.max(scores, axis=2, keepdims=True))
        log_total = highest + jnp.log(lax.optimization_barrier(jnp.sum(jnp.exp(scores - highest), axis=2, keepdims=True)))
        probs = jnp.where(allowed[None], jnp.exp(scores - log_total), 0.0)
        probs_low = probs.astype(jnp.bfloat16).astype(jnp.float32)
        attended = jnp.einsum('hqk,hkd->hqd', probs_low, near_v).astype(jnp.bfloat16)
        row_dot = lax.optimization_barrier(jnp.sum(own_g * attended.astype(jnp.float32), axis=2))
        prob_grad = jnp.einsum('hqd,hkd->hqk', own_g, near_v)
        score_grad = (probs * (prob_grad - row_dot[:, :, None])).astype(jnp.bfloat16).astype(jnp.float32)
        query_grad = (jnp.einsum('hqk,hkd->hqd', score_grad, near_k) * factor).astype(jnp.bfloat16)
        return (attended, log_total[:, :, 0], row_dot, query_grad)
    indices = jnp.arange(count_t * count_h, dtype=jnp.int32)
    attended, log_total, row_dot, query_grad = lax.map(forward, indices)
    query_pad = pad_tiles(query_blocks)
    grad_pad = pad_tiles(grad_blocks)
    total_pad = pad_tiles(log_total.reshape(count_t, count_h, HEADS, tokens))
    dot_pad = pad_tiles(row_dot.reshape(count_t, count_h, HEADS, tokens))

    def backward(index):
        first = index // count_h
        second = index % count_h
        allowed_back = window(first, second, count_t, count_h, tokens).T
        own_k = key_blocks[first, second].astype(jnp.float32)
        own_v = value_blocks[first, second].astype(jnp.float32)
        near_q = beside_all(query_pad, first, second).astype(jnp.float32)
        near_g = beside_all(grad_pad, first, second).astype(jnp.float32)
        near_total = beside_all(total_pad, first, second)
        near_dot = beside_all(dot_pad, first, second)
        scores = jnp.einsum('hqd,hkd->hqk', near_q, own_k) * factor
        probs = jnp.where(allowed_back[None], jnp.exp(scores - near_total[:, :, None]), 0.0)
        probs_low = probs.astype(jnp.bfloat16).astype(jnp.float32)
        value_grad = jnp.einsum('hqk,hqd->hkd', probs_low, near_g).astype(jnp.bfloat16)
        prob_grad = jnp.einsum('hqd,hkd->hqk', near_g, own_v)
        score_grad = (probs * (prob_grad - near_dot[:, :, None])).astype(jnp.bfloat16).astype(jnp.float32)
        key_grad = (jnp.einsum('hqk,hqd->hkd', score_grad, near_q) * factor).astype(jnp.bfloat16)
        return (key_grad, value_grad)
    key_grad, value_grad = lax.map(backward, indices)
    shape_back = (count_t, count_h, HEADS, tokens, DH)
    return (from_blocks(attended.reshape(shape_back), count_t, count_h, columns), from_blocks(query_grad.reshape(shape_back), count_t, count_h, columns), from_blocks(key_grad.reshape(shape_back), count_t, count_h, columns), from_blocks(value_grad.reshape(shape_back), count_t, count_h, columns))
```

```python
import functools
import math

import jax
import jax.numpy as jnp
from jax import lax
from jax.experimental import pallas as pl
from jax.experimental.pallas import tpu as pltpu
from jax.sharding import PartitionSpec as P

DH = 128
LOW = -1e30


def neighbours(axis, size):
    me = lax.axis_index(axis)
    if size == 1:
        return []
    if size == 2:
        return [(1 - me, None, 1)]
    return [(me - 1, me > 0, 2), (me + 1, me < size - 1, 1)]


def guarded(valid, fn):
    if valid is None:
        fn()
    else:
        pl.when(valid)(fn)


def kernel(
    sizes,
    rows,
    heads,
    q_ref,
    k_ref,
    v_ref,
    g_ref,
    o_ref,
    dq_ref,
    dk_ref,
    dv_ref,
    qg,
    win,
    s_ref,
    outb,
    own,
    r1s,
    r1r,
    r2s,
    r2r,
    in_s,
    in_r,
    ht_s,
    ht_r,
    hh_s,
    hh_r,
    a1_s,
    a1_r,
    a2_s,
    a2_r,
    ou_s,
    ou_r,
):
    size_t, size_h, size_z = sizes
    tokens = rows * size_z
    z = lax.axis_index("head")
    times = neighbours("ta", size_t)
    sides = neighbours("ha", size_h)
    nt, nr = 1 + len(times), 1 + len(sides)
    factor = 1.0 / math.sqrt(DH)
    scale = factor * math.log2(math.e)

    barrier = pltpu.get_barrier_semaphore()
    expected = size_z - 1
    for d in range(1, size_z):
        pl.semaphore_signal(barrier, inc=1, device_id={"head": lax.rem(z + d, size_z)}, device_id_type=pl.DeviceIdType.MESH)
    for axis, near in (("ta", times), ("ha", sides)):
        for peer, valid, _ in near:

            def greet(axis=axis, peer=peer):
                pl.semaphore_signal(barrier, inc=1, device_id={axis: peer}, device_id_type=pl.DeviceIdType.MESH)

            guarded(valid, greet)
            expected = expected + (1 if valid is None else jnp.where(valid, 1, 0))
    pl.semaphore_wait(barrier, expected)

    def columns(group, h):
        return pl.ds(pl.multiple_of((group * heads + h) * DH, DH), DH)

    def part(group):
        return pl.ds(pl.multiple_of(group * rows, rows), rows)

    ins = (k_ref, v_ref, q_ref, g_ref)
    outs = (o_ref, dq_ref, dk_ref, dv_ref)

    def landing(h, a, group):
        if a < 2:
            return win.at[h, 0, 0, a, part(group), :]
        return qg.at[h, a - 2, part(group), :]

    def in_copy(h, a, d):
        peer = lax.rem(z + d, size_z)
        return pltpu.make_async_remote_copy(
            src_ref=ins[a].at[:, columns(peer, h)],
            dst_ref=landing(h, a, z),
            send_sem=in_s.at[h, a, d],
            recv_sem=in_r.at[h, a, d],
            device_id={"head": peer},
            device_id_type=pl.DeviceIdType.MESH,
        )

    def out_copy(h, a, d):
        peer = lax.rem(z + d, size_z)
        return pltpu.make_async_remote_copy(
            src_ref=outb.at[h, a, part(peer), :],
            dst_ref=outs[a].at[:, columns(z, h)],
            send_sem=ou_s.at[h, a, d],
            recv_sem=ou_r.at[h, a, d],
            device_id={"head": peer},
            device_id_type=pl.DeviceIdType.MESH,
        )

    def side_copy(axis, src, dst, send, recv, peer):
        return pltpu.make_async_remote_copy(
            src_ref=src,
            dst_ref=dst,
            send_sem=send,
            recv_sem=recv,
            device_id={axis: peer},
            device_id_type=pl.DeviceIdType.MESH,
        )

    def halo_t(h, i):
        peer, _, there = times[i]
        return side_copy("ta", win.at[h, 0, 0], win.at[h, 0, there], ht_s.at[h, i], ht_r.at[h, there - 1], peer)

    def halo_h(h, i):
        peer, _, there = sides[i]
        return side_copy("ha", win.at[h, 0], win.at[h, there], hh_s.at[h, i], hh_r.at[h, there - 1], peer)

    def back_h(h, i):
        peer, _, there = sides[i]
        return side_copy("ha", r1s.at[h, i], r1r.at[h, there - 1], a1_s.at[h, i], a1_r.at[h, there - 1], peer)

    def back_t(h, i):
        peer, _, there = times[i]
        return side_copy("ta", r2s.at[h, i], r2r.at[h, there - 1], a2_s.at[h, i], a2_r.at[h, there - 1], peer)

    def arrival(axis, dst, recv, peer):
        return side_copy(axis, dst, dst, recv, recv, peer)

    for i, (peer, valid, _) in enumerate(times):
        if valid is not None:

            @pl.when(jnp.logical_not(valid))
            def _(i=i):
                @pl.loop(0, heads)
                def _(h):
                    win[h, 0, i + 1] = jnp.zeros((2, tokens, DH), win.dtype)

    for i, (peer, valid, _) in enumerate(sides):
        if valid is not None:

            @pl.when(jnp.logical_not(valid))
            def _(i=i):
                @pl.loop(0, heads)
                def _(h):
                    win[h, i + 1] = jnp.zeros((nt, 2, tokens, DH), win.dtype)

    @pl.loop(0, heads)
    def _(h):
        for a in range(4):
            for d in range(1, size_z):
                in_copy(h, a, d).start()
        for a in range(4):
            landing(h, a, z)[...] = ins[a][:, columns(z, h)]

    def send_times(h):
        for a in range(2):
            for d in range(1, size_z):
                in_copy(h, a, d).wait_recv()
        for i, (peer, valid, _) in enumerate(times):
            guarded(valid, lambda i=i: halo_t(h, i).start())

    def send_sides(h):
        for i, (peer, valid, _) in enumerate(times):
            guarded(valid, lambda i=i, peer=peer: arrival("ta", win.at[h, 0, i + 1], ht_r.at[h, i], peer).wait_recv())
        for i, (peer, valid, _) in enumerate(sides):
            guarded(valid, lambda i=i: halo_h(h, i).start())

    def attend(h):
        for a in range(2, 4):
            for d in range(1, size_z):
                in_copy(h, a, d).wait_recv()
        queries = qg[h, 0]
        grads = qg[h, 1]
        highest = jnp.full((1, tokens), LOW, jnp.float32)
        for r in range(nr):
            if r > 0:
                peer, valid, _ = sides[r - 1]
                guarded(valid, lambda r=r, peer=peer: arrival("ha", win.at[h, r], hh_r.at[h, r - 1], peer).wait_recv())
            for t in range(nt):
                scores = lax.dot_general(win[h, r, t, 0], queries, (((1,), (1,)), ((), ())), preferred_element_type=jnp.float32) * scale
                for cond in ([times[t - 1][1]] if t > 0 else []) + ([sides[r - 1][1]] if r > 0 else []):
                    if cond is not None:
                        scores = jnp.where(cond, scores, LOW)
                s_ref[r * nt + t] = scores
                highest = jnp.maximum(highest, jnp.max(scores, axis=0, keepdims=True))
        total = jnp.zeros((1, tokens), jnp.float32)
        mixed = jnp.zeros((DH, tokens), jnp.float32)
        for r in range(nr):
            for t in range(nt):
                weights = jnp.exp2(s_ref[r * nt + t] - highest)
                s_ref[r * nt + t] = weights
                total = total + jnp.sum(weights, axis=0, keepdims=True)
                mixed = mixed + lax.dot_general(
                    win[h, r, t, 1], weights.astype(jnp.bfloat16), (((0,), (0,)), ((), ())), preferred_element_type=jnp.float32
                )
        inverse = 1.0 / total
        attended = jnp.transpose(mixed * inverse).astype(jnp.bfloat16)
        outb[h, 0] = attended
        products = grads.astype(jnp.float32) * attended.astype(jnp.float32)
        row_dot = jnp.sum(jnp.transpose(products), axis=0, keepdims=True)
        for d in range(1, size_z):
            out_copy(h, 0, d).start()
        query_grad = jnp.zeros((DH, tokens), jnp.float32)
        for r in reversed(range(nr)):
            for t in range(nt):
                keys, values = win[h, r, t, 0], win[h, r, t, 1]
                probs = s_ref[r * nt + t] * inverse
                value_term = jnp.dot(probs.astype(jnp.bfloat16), grads, preferred_element_type=jnp.float32)
                prob_grad = lax.dot_general(values, grads, (((1,), (1,)), ((), ())), preferred_element_type=jnp.float32)
                score_grad = (probs * (prob_grad - row_dot)).astype(jnp.bfloat16)
                query_grad = query_grad + lax.dot_general(
                    keys, score_grad, (((0,), (0,)), ((), ())), preferred_element_type=jnp.float32
                )
                key_term = jnp.dot(score_grad, queries, preferred_element_type=jnp.float32) * factor
                if r == 0:
                    own[h, t, 0] = key_term
                    own[h, t, 1] = value_term
                else:
                    r1s[h, r - 1, t, 0] = key_term.astype(jnp.bfloat16)
                    r1s[h, r - 1, t, 1] = value_term.astype(jnp.bfloat16)
            if r > 0:
                guarded(sides[r - 1][1], lambda r=r: back_h(h, r - 1).start())
        outb[h, 1] = jnp.transpose(query_grad * factor).astype(jnp.bfloat16)
        for d in range(1, size_z):
            out_copy(h, 1, d).start()

    def return_times(h):
        for i, (peer, valid, _) in enumerate(sides):

            def fold(i=i, peer=peer):
                arrival("ha", r1r.at[h, i], a1_r.at[h, i], peer).wait_recv()
                for t in range(nt):
                    own[h, t] = own[h, t] + r1r[h, i, t].astype(jnp.float32)

            guarded(valid, fold)
        for i, (peer, valid, _) in enumerate(times):

            def send(i=i):
                r2s[h, i] = own[h, i + 1].astype(jnp.bfloat16)
                back_t(h, i).start()

            guarded(valid, send)

    def finish(h):
        for i, (peer, valid, _) in enumerate(times):

            def fold(i=i, peer=peer):
                arrival("ta", r2r.at[h, i], a2_r.at[h, i], peer).wait_recv()
                own[h, 0] = own[h, 0] + r2r[h, i].astype(jnp.float32)

            guarded(valid, fold)
        outb[h, 2] = own[h, 0, 0].astype(jnp.bfloat16)
        outb[h, 3] = own[h, 0, 1].astype(jnp.bfloat16)
        for a in range(2, 4):
            for d in range(1, size_z):
                out_copy(h, a, d).start()
        for a in range(4):
            outs[a][:, columns(z, h)] = outb[h, a, part(z), :]

    send_times(0)

    @pl.loop(0, heads)
    def _(h):
        pl.when(h + 1 < heads)(lambda: send_times(h + 1))
        send_sides(h)
        attend(h)
        return_times(h)
        pl.when(h > 0)(lambda: finish(h - 1))

    finish(heads - 1)

    @pl.loop(0, heads)
    def _(h):
        for a in range(4):
            for d in range(1, size_z):
                in_copy(h, a, d).wait_send()
                out_copy(h, a, d).wait_recv()
                out_copy(h, a, d).wait_send()
        for i, (peer, valid, _) in enumerate(times):
            guarded(valid, lambda i=i: halo_t(h, i).wait_send())
            guarded(valid, lambda i=i: back_t(h, i).wait_send())
        for i, (peer, valid, _) in enumerate(sides):
            guarded(valid, lambda i=i: halo_h(h, i).wait_send())
            guarded(valid, lambda i=i: back_h(h, i).wait_send())


def body(queries, keys, values, out_grad):
    sizes = tuple(lax.axis_size(axis) for axis in ("ta", "ha", "head"))
    size_t, size_h, size_z = sizes
    shape = queries.shape
    rows = shape[0] * shape[1] * shape[2]
    width = shape[3]
    heads = width // DH // size_z
    tokens = rows * size_z
    nt, nr = min(3, size_t), min(3, size_h)
    bf16 = jnp.bfloat16
    dma = pltpu.SemaphoreType.DMA
    mt, mr = max(1, nt - 1), max(1, nr - 1)
    flat = [x.reshape(rows, width) for x in (queries, keys, values, out_grad)]
    outs = pl.pallas_call(
        functools.partial(kernel, sizes, rows, heads),
        out_shape=[jax.ShapeDtypeStruct((rows, width), bf16)] * 4,
        in_specs=[pl.BlockSpec(memory_space=pltpu.VMEM)] * 4,
        out_specs=[pl.BlockSpec(memory_space=pltpu.VMEM)] * 4,
        scratch_shapes=[
            pltpu.VMEM((heads, 2, tokens, DH), bf16),
            pltpu.VMEM((heads, nr, nt, 2, tokens, DH), bf16),
            pltpu.VMEM((nr * nt, tokens, tokens), jnp.float32),
            pltpu.VMEM((heads, 4, tokens, DH), bf16),
            pltpu.VMEM((heads, nt, 2, tokens, DH), jnp.float32),
            pltpu.VMEM((heads, mr, nt, 2, tokens, DH), bf16),
            pltpu.VMEM((heads, mr, nt, 2, tokens, DH), bf16),
            pltpu.VMEM((heads, mt, 2, tokens, DH), bf16),
            pltpu.VMEM((heads, mt, 2, tokens, DH), bf16),
            dma((heads, 4, size_z)),
            dma((heads, 4, size_z)),
            dma((heads, mt)),
            dma((heads, mt)),
            dma((heads, mr)),
            dma((heads, mr)),
            dma((heads, mr)),
            dma((heads, mr)),
            dma((heads, mt)),
            dma((heads, mt)),
            dma((heads, 4, size_z)),
            dma((heads, 4, size_z)),
        ],
        compiler_params=pltpu.CompilerParams(collective_id=0, has_side_effects=True, vmem_limit_bytes=56 * 1024 * 1024),
        name="tile_attention",
    )(*flat)
    return tuple(x.reshape(shape) for x in outs)


def solution(mesh):
    spec = P("ta", ("ha", "head"), None, None)
    return jax.shard_map(body, mesh=mesh, in_specs=(spec,) * 4, out_specs=(spec,) * 4, check_vma=False)
```

```python
import functools
import math

import jax
import jax.numpy as jnp
from jax import lax
from jax.experimental import pallas as pl
from jax.experimental.pallas import tpu as pltpu
from jax.sharding import PartitionSpec as P

DH = 128
LOW = -1e30


def neighbours(axis, size):
    me = lax.axis_index(axis)
    if size == 1:
        return []
    if size == 2:
        return [(1 - me, None, 1)]
    return [(me - 1, me > 0, 2), (me + 1, me < size - 1, 1)]


def guarded(valid, fn):
    if valid is None:
        fn()
    else:
        pl.when(valid)(fn)


def kernel(
    sizes,
    rows,
    heads,
    q_ref,
    k_ref,
    v_ref,
    g_ref,
    o_ref,
    dq_ref,
    dk_ref,
    dv_ref,
    qg,
    win,
    s_ref,
    outb,
    own,
    r1s,
    r1r,
    r2s,
    r2r,
    in_s,
    in_r,
    ht_s,
    ht_r,
    hh_s,
    hh_r,
    a1_s,
    a1_r,
    a2_s,
    a2_r,
    ou_s,
    ou_r,
):
    size_t, size_h, size_z = sizes
    tokens = rows * size_z
    z = lax.axis_index("head")
    times = neighbours("ta", size_t)
    sides = neighbours("ha", size_h)
    nt, nr = 1 + len(times), 1 + len(sides)
    relay = size_t == 4
    step = lax.axis_index("ta")
    across, along = step + 1 - 2 * lax.rem(step, 2), lax.rem(step + 2, 4)
    near, far = 2 - lax.rem(step, 2), 1 + lax.rem(step, 2)
    inner = (step == 1) | (step == 2)
    outer = jnp.logical_not(inner)
    greeted = [(across, None, None), (along, None, None)] if relay else times
    factor = 1.0 / math.sqrt(DH)
    scale = factor * math.log2(math.e)

    barrier = pltpu.get_barrier_semaphore()
    expected = size_z - 1
    for d in range(1, size_z):
        pl.semaphore_signal(barrier, inc=1, device_id={"head": lax.rem(z + d, size_z)}, device_id_type=pl.DeviceIdType.MESH)
    for axis, group in (("ta", greeted), ("ha", sides)):
        for peer, valid, _ in group:

            def greet(axis=axis, peer=peer):
                pl.semaphore_signal(barrier, inc=1, device_id={axis: peer}, device_id_type=pl.DeviceIdType.MESH)

            guarded(valid, greet)
            expected = expected + (1 if valid is None else jnp.where(valid, 1, 0))
    pl.semaphore_wait(barrier, expected)

    def columns(group, h):
        return pl.ds(pl.multiple_of((group * heads + h) * DH, DH), DH)

    def part(group):
        return pl.ds(pl.multiple_of(group * rows, rows), rows)

    ins = (k_ref, v_ref, q_ref, g_ref)
    outs = (o_ref, dq_ref, dk_ref, dv_ref)

    def landing(h, a, group):
        if a < 2:
            return win.at[h, 0, 0, a, part(group), :]
        return qg.at[h, a - 2, part(group), :]

    def in_copy(h, a, d):
        peer = lax.rem(z + d, size_z)
        return pltpu.make_async_remote_copy(
            src_ref=ins[a].at[:, columns(peer, h)],
            dst_ref=landing(h, a, z),
            send_sem=in_s.at[h, a, d],
            recv_sem=in_r.at[h, a, d],
            device_id={"head": peer},
            device_id_type=pl.DeviceIdType.MESH,
        )

    def out_copy(h, a, d):
        peer = lax.rem(z + d, size_z)
        return pltpu.make_async_remote_copy(
            src_ref=outb.at[h, a, part(peer), :],
            dst_ref=outs[a].at[:, columns(z, h)],
            send_sem=ou_s.at[h, a, d],
            recv_sem=ou_r.at[h, a, d],
            device_id={"head": peer},
            device_id_type=pl.DeviceIdType.MESH,
        )

    def side_copy(axis, src, dst, send, recv, peer):
        return pltpu.make_async_remote_copy(
            src_ref=src,
            dst_ref=dst,
            send_sem=send,
            recv_sem=recv,
            device_id={axis: peer},
            device_id_type=pl.DeviceIdType.MESH,
        )

    def halo_t(h, i):
        peer, _, there = times[i]
        return side_copy("ta", win.at[h, 0, 0], win.at[h, 0, there], ht_s.at[h, i], ht_r.at[h, there - 1], peer)

    def halo_across(h):
        return side_copy("ta", win.at[h, 0, 0], win.at[h, 0, far], ht_s.at[h, 0], ht_r.at[h, far - 1], across)

    def halo_along(h):
        return side_copy("ta", win.at[h, 0, near], win.at[h, 0, far], ht_s.at[h, 1], ht_r.at[h, far - 1], along)

    def back_across(h):
        return side_copy("ta", r2s.at[h, 0], r2r.at[h, 0], a2_s.at[h, 0], a2_r.at[h, 0], across)

    def back_along(h):
        return side_copy("ta", r2s.at[h, 1], r2r.at[h, 1], a2_s.at[h, 1], a2_r.at[h, 1], along)

    def halo_h(h, i):
        peer, _, there = sides[i]
        return side_copy("ha", win.at[h, 0], win.at[h, there], hh_s.at[h, i], hh_r.at[h, there - 1], peer)

    def back_h(h, i):
        peer, _, there = sides[i]
        return side_copy("ha", r1s.at[h, i], r1r.at[h, there - 1], a1_s.at[h, i], a1_r.at[h, there - 1], peer)

    def back_t(h, i):
        peer, _, there = times[i]
        return side_copy("ta", r2s.at[h, i], r2r.at[h, there - 1], a2_s.at[h, i], a2_r.at[h, there - 1], peer)

    def arrival(axis, dst, recv, peer):
        return side_copy(axis, dst, dst, recv, recv, peer)

    for i, (peer, valid, _) in enumerate(times):
        if valid is not None:

            @pl.when(jnp.logical_not(valid))
            def _(i=i):
                @pl.loop(0, heads)
                def _(h):
                    win[h, 0, i + 1] = jnp.zeros((2, tokens, DH), win.dtype)

    for i, (peer, valid, _) in enumerate(sides):
        if valid is not None:

            @pl.when(jnp.logical_not(valid))
            def _(i=i):
                @pl.loop(0, heads)
                def _(h):
                    win[h, i + 1] = jnp.zeros((nt, 2, tokens, DH), win.dtype)

    def send_in(h, first):
        for a in (first, first + 1):
            for d in range(1, size_z):
                in_copy(h, a, d).start()

    send_in(0, 0)

    @pl.loop(0, heads)
    def _(h):
        pl.when(h + 1 < heads)(lambda: send_in(h + 1, 0))
        send_in(h, 2)

    @pl.loop(0, heads)
    def _(h):
        for a in range(4):
            landing(h, a, z)[...] = ins[a][:, columns(z, h)]

    def send_times(h):
        for a in range(2):
            for d in range(1, size_z):
                in_copy(h, a, d).wait_recv()
        if relay:
            halo_across(h).start()
            return
        for i, (peer, valid, _) in enumerate(times):
            guarded(valid, lambda i=i: halo_t(h, i).start())

    def pass_on(h):
        if relay:
            arrival("ta", win.at[h, 0, near], ht_r.at[h, near - 1], across).wait_recv()
            pl.when(outer)(lambda: halo_along(h).start())

    def send_sides(h):
        if relay:
            pl.when(inner)(lambda: arrival("ta", win.at[h, 0, far], ht_r.at[h, far - 1], along).wait_recv())
        else:
            for i, (peer, valid, _) in enumerate(times):
                guarded(valid, lambda i=i, peer=peer: arrival("ta", win.at[h, 0, i + 1], ht_r.at[h, i], peer).wait_recv())
        for i, (peer, valid, _) in enumerate(sides):
            guarded(valid, lambda i=i: halo_h(h, i).start())

    def attend(h, between):
        for a in range(2, 4):
            for d in range(1, size_z):
                in_copy(h, a, d).wait_recv()
        queries = qg[h, 0]
        grads = qg[h, 1]
        highest = jnp.full((1, tokens), LOW, jnp.float32)
        for r in range(nr):
            if r > 0:
                peer, valid, _ = sides[r - 1]
                guarded(valid, lambda r=r, peer=peer: arrival("ha", win.at[h, r], hh_r.at[h, r - 1], peer).wait_recv())
            for t in range(nt):
                scores = lax.dot_general(win[h, r, t, 0], queries, (((1,), (1,)), ((), ())), preferred_element_type=jnp.float32) * scale
                for cond in ([times[t - 1][1]] if t > 0 else []) + ([sides[r - 1][1]] if r > 0 else []):
                    if cond is not None:
                        scores = jnp.where(cond, scores, LOW)
                s_ref[r * nt + t] = scores
                highest = jnp.maximum(highest, jnp.max(scores, axis=0, keepdims=True))
        total = jnp.zeros((1, tokens), jnp.float32)
        mixed = jnp.zeros((DH, tokens), jnp.float32)
        for r in range(nr):
            for t in range(nt):
                weights = jnp.exp2(s_ref[r * nt + t] - highest)
                s_ref[r * nt + t] = weights
                total = total + jnp.sum(weights, axis=0, keepdims=True)
                mixed = mixed + lax.dot_general(
                    win[h, r, t, 1], weights.astype(jnp.bfloat16), (((0,), (0,)), ((), ())), preferred_element_type=jnp.float32
                )
        inverse = 1.0 / total
        attended = jnp.transpose(mixed * inverse).astype(jnp.bfloat16)
        outb[h, 0] = attended
        products = grads.astype(jnp.float32) * attended.astype(jnp.float32)
        row_dot = jnp.sum(jnp.transpose(products), axis=0, keepdims=True)
        for d in range(1, size_z):
            out_copy(h, 0, d).start()
        between()
        query_grad = jnp.zeros((DH, tokens), jnp.float32)
        for r in reversed(range(nr)):
            for t in range(nt):
                keys, values = win[h, r, t, 0], win[h, r, t, 1]
                probs = s_ref[r * nt + t] * inverse
                value_term = jnp.dot(probs.astype(jnp.bfloat16), grads, preferred_element_type=jnp.float32)
                prob_grad = lax.dot_general(values, grads, (((1,), (1,)), ((), ())), preferred_element_type=jnp.float32)
                score_grad = (probs * (prob_grad - row_dot)).astype(jnp.bfloat16)
                query_grad = query_grad + lax.dot_general(
                    keys, score_grad, (((0,), (0,)), ((), ())), preferred_element_type=jnp.float32
                )
                key_term = jnp.dot(score_grad, queries, preferred_element_type=jnp.float32) * factor
                if r == 0:
                    own[h, t, 0] = key_term
                    own[h, t, 1] = value_term
                else:
                    r1s[h, r - 1, t, 0] = key_term.astype(jnp.bfloat16)
                    r1s[h, r - 1, t, 1] = value_term.astype(jnp.bfloat16)
            if r > 0:
                guarded(sides[r - 1][1], lambda r=r: back_h(h, r - 1).start())
        outb[h, 1] = jnp.transpose(query_grad * factor).astype(jnp.bfloat16)
        for d in range(1, size_z):
            out_copy(h, 1, d).start()

    def return_times(h):
        for i, (peer, valid, _) in enumerate(sides):

            def fold(i=i, peer=peer):
                arrival("ha", r1r.at[h, i], a1_r.at[h, i], peer).wait_recv()
                for t in range(nt):
                    own[h, t] = own[h, t] + r1r[h, i, t].astype(jnp.float32)

            guarded(valid, fold)
        if relay:

            @pl.when(inner)
            def _():
                r2s[h, 1] = own[h, far].astype(jnp.bfloat16)
                back_along(h).start()
                r2s[h, 0] = own[h, near].astype(jnp.bfloat16)
                back_across(h).start()

            return
        for i, (peer, valid, _) in enumerate(times):

            def send(i=i):
                r2s[h, i] = own[h, i + 1].astype(jnp.bfloat16)
                back_t(h, i).start()

            guarded(valid, send)

    def pass_back(h):
        if relay:

            @pl.when(outer)
            def _():
                arrival("ta", r2r.at[h, 1], a2_r.at[h, 1], along).wait_recv()
                r2s[h, 0] = (own[h, near] + r2r[h, 1].astype(jnp.float32)).astype(jnp.bfloat16)
                back_across(h).start()

    def finish(h):
        if relay:
            arrival("ta", r2r.at[h, 0], a2_r.at[h, 0], across).wait_recv()
            own[h, 0] = own[h, 0] + r2r[h, 0].astype(jnp.float32)
        else:
            for i, (peer, valid, _) in enumerate(times):

                def fold(i=i, peer=peer):
                    arrival("ta", r2r.at[h, i], a2_r.at[h, i], peer).wait_recv()
                    own[h, 0] = own[h, 0] + r2r[h, i].astype(jnp.float32)

                guarded(valid, fold)
        outb[h, 2] = own[h, 0, 0].astype(jnp.bfloat16)
        outb[h, 3] = own[h, 0, 1].astype(jnp.bfloat16)
        for a in range(2, 4):
            for d in range(1, size_z):
                out_copy(h, a, d).start()
        for a in range(4):
            outs[a][:, columns(z, h)] = outb[h, a, part(z), :]

    send_times(0)
    pass_on(0)

    @pl.loop(0, heads)
    def _(h):
        pl.when(h + 1 < heads)(lambda: send_times(h + 1))
        send_sides(h)
        pl.when(h + 1 < heads)(lambda: pass_on(h + 1))
        pl.when(h > 0)(lambda: pass_back(h - 1))
        attend(h, lambda: pl.when(h > 0)(lambda: finish(h - 1)))
        return_times(h)

    pass_back(heads - 1)
    finish(heads - 1)

    @pl.loop(0, heads)
    def _(h):
        for a in range(4):
            for d in range(1, size_z):
                in_copy(h, a, d).wait_send()
                out_copy(h, a, d).wait_recv()
                out_copy(h, a, d).wait_send()
        if relay:
            halo_across(h).wait_send()
            back_across(h).wait_send()
            pl.when(outer)(lambda: halo_along(h).wait_send())
            pl.when(inner)(lambda: back_along(h).wait_send())
        else:
            for i, (peer, valid, _) in enumerate(times):
                guarded(valid, lambda i=i: halo_t(h, i).wait_send())
                guarded(valid, lambda i=i: back_t(h, i).wait_send())
        for i, (peer, valid, _) in enumerate(sides):
            guarded(valid, lambda i=i: halo_h(h, i).wait_send())
            guarded(valid, lambda i=i: back_h(h, i).wait_send())


def body(queries, keys, values, out_grad):
    sizes = tuple(lax.axis_size(axis) for axis in ("ta", "ha", "head"))
    size_t, size_h, size_z = sizes
    shape = queries.shape
    rows = shape[0] * shape[1] * shape[2]
    width = shape[3]
    heads = width // DH // size_z
    tokens = rows * size_z
    nt, nr = min(3, size_t), min(3, size_h)
    bf16 = jnp.bfloat16
    dma = pltpu.SemaphoreType.DMA
    mt, mr = max(1, nt - 1), max(1, nr - 1)
    flat = [x.reshape(rows, width) for x in (queries, keys, values, out_grad)]
    outs = pl.pallas_call(
        functools.partial(kernel, sizes, rows, heads),
        out_shape=[jax.ShapeDtypeStruct((rows, width), bf16)] * 4,
        in_specs=[pl.BlockSpec(memory_space=pltpu.VMEM)] * 4,
        out_specs=[pl.BlockSpec(memory_space=pltpu.VMEM)] * 4,
        scratch_shapes=[
            pltpu.VMEM((heads, 2, tokens, DH), bf16),
            pltpu.VMEM((heads, nr, nt, 2, tokens, DH), bf16),
            pltpu.VMEM((nr * nt, tokens, tokens), jnp.float32),
            pltpu.VMEM((heads, 4, tokens, DH), bf16),
            pltpu.VMEM((heads, nt, 2, tokens, DH), jnp.float32),
            pltpu.VMEM((heads, mr, nt, 2, tokens, DH), bf16),
            pltpu.VMEM((heads, mr, nt, 2, tokens, DH), bf16),
            pltpu.VMEM((heads, mt, 2, tokens, DH), bf16),
            pltpu.VMEM((heads, mt, 2, tokens, DH), bf16),
            dma((heads, 4, size_z)),
            dma((heads, 4, size_z)),
            dma((heads, mt)),
            dma((heads, mt)),
            dma((heads, mr)),
            dma((heads, mr)),
            dma((heads, mr)),
            dma((heads, mr)),
            dma((heads, mt)),
            dma((heads, mt)),
            dma((heads, 4, size_z)),
            dma((heads, 4, size_z)),
        ],
        compiler_params=pltpu.CompilerParams(collective_id=0, has_side_effects=True, vmem_limit_bytes=56 * 1024 * 1024),
        name="tile_attention",
    )(*flat)
    return tuple(x.reshape(shape) for x in outs)


def solution(mesh):
    spec = P("ta", ("ha", "head"), None, None)
    return jax.shard_map(body, mesh=mesh, in_specs=(spec,) * 4, out_specs=(spec,) * 4, check_vma=False)
```
